32 devices in a mesh: heads: 4 (over y, x), docs: 8 (over z, core).
Axes of the slice: x: 2, y: 2, z: 4, core: 2. Of those that a mesh axis runs over, the one named last changes fastest.
Arguments:
- query_rows: bfloat16 [4096, 4096], P('docs', 'heads'), may hold values from -40 to 40
- key_rows: bfloat16 [4096, 512], P('docs', 'heads'), may hold values from -4.5 to 4.5
- value_rows: bfloat16 [4096, 512], P('docs', 'heads'), may hold values from -6 to 6
- doc_blocks: int32 [4], replicated, may hold values from 1 to 16, 32 in all
- out_weight: bfloat16 [4096, 2048], P('heads', 'docs'), may hold values from -0.125 to 0.125
Outputs:
- mixed: bfloat16 [4096, 2048], P('docs', 'heads')
The draws below stay inside these ranges and needn't reach their ends.
All inputs are finite; a program needn't handle non-finite values.
Results may differ from the reference program's by a relative error of at most 0.0095.
Values may be sent and summed in bfloat16 or wider, within the bound.
No kernel may reach another device: no remote copies, remote signals or barrier semaphores. Data moves between devices by JAX's collectives and lax.ppermute only.
A program may use at most 64 MiB of HBM per device.

```python
import math
import jax
import jax.numpy as jnp
import numpy as np
from jax import lax

D_MODEL = 2048
QH = 32
KVH = 4
HD = 128
BLOCK = 128
MOSTB = 16
TOK_DEV = 512
TOKENS = 4096
NBLK = 32
NDOC = 4
N_HEADS = 4


def shared_rows(key):
    base = jax.random.fold_in(key, 7)
    first_key, second_key = jax.random.split(base, 2)
    key_draw = jnp.clip(jax.random.normal(first_key, (TOKENS, KVH * HD), jnp.float32), -4.0, 4.0)
    query_draw = jnp.clip(jax.random.normal(second_key, (TOKENS, QH * HD), jnp.float32), -4.0, 4.0)
    return (query_draw, key_draw)


def draw_query_rows(key, part):
    return shared_rows(key)[0].astype(jnp.bfloat16)


def draw_key_rows(key, part):
    return shared_rows(key)[1].astype(jnp.bfloat16)


def with_spikes(array, rng, source, target, shards_of, factor):
    owner, partner = [(jnp.arange(array.shape[axis_at]) // (array.shape[axis_at] // shards_of)).reshape([-1 if axis == axis_at else 1 for axis in range(array.ndim)]) for axis_at in (source, target)]
    chosen = jax.random.permutation(rng, shards_of)[partner]
    strong = (owner == chosen) | (owner == (partner + shards_of // 2) % shards_of)
    return jnp.where(strong, factor * array, array)


def block_scale(own_key, shape, pieces, low, top_value):
    loudness = 1.0
    for axis_at, blocks in pieces:
        steps = jax.random.uniform(jax.random.fold_in(jax.random.fold_in(own_key, 6), axis_at), (blocks,), jnp.float32, low / len(pieces), top_value / len(pieces))
        loudness = loudness * jnp.repeat(jnp.exp(steps), shape[axis_at] // blocks).reshape((-1,) + (1,) * (len(shape) - 1 - axis_at))
    return loudness


def split_up(number_of, total, limit, skew):
    loads = [(1 << 20) // math.isqrt(standing ** skew) + 1 for standing in range(2, number_of + 1)]
    spare, holding = total - limit - (number_of - 1), [1] * (number_of - 1)
    while spare > 0:
        candidates = [i for i in range(number_of - 1) if holding[i] < limit]
        whole, left = sum([loads[i] for i in candidates]), spare
        for i in candidates:
            addition = min(limit - holding[i], max(1, left * loads[i] // whole), spare)
            holding[i] = holding[i] + addition
            spare = spare - addition
    return np.array([limit] + holding)


def ragged_sizes(rng, count, total, limit, skew):
    if count == 2:
        one = jax.random.randint(rng, (), max(1, total - limit), min(limit, total - 1) + 1)
        return jnp.stack([one, total - one])
    lengths = jnp.asarray(split_up(count, total, limit, skew), jnp.int32)
    couples = (count - 1) // 2
    giver, receiver = lengths[1:1 + 2 * couples:2], lengths[2:2 + 2 * couples:2]
    room = jnp.minimum(giver - 1, limit - receiver)
    moved = jax.random.randint(jax.random.fold_in(rng, 1), (couples,), 0, 1 << 20) % (room + 1)
    lengths = lengths.at[1:1 + 2 * couples:2].set(giver - moved).at[2:2 + 2 * couples:2].set(receiver + moved)
    return lengths[jax.random.permutation(jax.random.fold_in(rng, 2), count)]


def noise(key, dims, scale, reach, cuts=(), kind=jnp.bfloat16):
    values = jax.random.normal(key, dims, jnp.float32) * scale
    if len(cuts) > 0:
        values = block_scale(key, dims, cuts, -0.22, 0.18) * values
    return jnp.clip(values, min=-reach, max=reach).astype(kind)


def noise_with(own_key, extent, spread, reach, cuts, heavy, kind=jnp.bfloat16):
    array = spread * jax.random.normal(own_key, extent, jnp.float32)
    if cuts:
        array = array * block_scale(own_key, extent, cuts, -0.22, 0.18)
    return jnp.clip(with_spikes(array, jax.random.fold_in(own_key, 3), *heavy), -reach, reach).astype(kind)


def setup_inputs(seed: int = 0) -> dict:
    arg_keys = jax.random.split(jax.random.key(seed), 6)
    return {
        "query_rows": draw_query_rows(jax.random.fold_in(arg_keys[5], 71), 0),
        "key_rows": draw_key_rows(jax.random.fold_in(arg_keys[5], 71), 0),
        "value_rows": noise(arg_keys[2], (TOKENS, KVH * HD), 1.0, 6.0, ((0, 8), (1, 4))),
        "doc_blocks": ragged_sizes(arg_keys[3], NDOC, NBLK, MOSTB, 2).astype(jnp.int32),
        "out_weight": noise_with(arg_keys[4], (QH * HD, D_MODEL), (QH * HD) ** -0.5, 0.125, ((0, 4), (1, 8)), (0, 1, 8, 2.0)),
    }


def reference(query_rows, key_rows, value_rows, doc_blocks, out_weight):
    token_count = query_rows.shape[0]
    rim_rows = (MOSTB - 1) * BLOCK
    query_block = min(512, TOK_DEV)
    window = rim_rows + query_block
    group_size = QH // KVH
    score_scale = HD ** -0.5
    doc_ends = jnp.cumsum(doc_blocks).astype(jnp.int32) * BLOCK
    positions = jnp.arange(token_count + rim_rows, dtype=jnp.int32) - rim_rows
    doc_ids = jnp.sum((doc_ends[None, :] <= positions[:, None]).astype(jnp.int32), axis=1)
    doc_ids = jnp.where(positions < 0, -1, doc_ids).astype(jnp.int32)
    padding = jnp.zeros((rim_rows, KVH * HD), key_rows.dtype)
    ext_keys = jnp.concatenate([padding, key_rows], axis=0)
    ext_values = jnp.concatenate([padding, value_rows], axis=0)

    def one_block(block_index):
        first_row = (block_index * query_block).astype(jnp.int32)
        query_part = lax.dynamic_slice_in_dim(query_rows, first_row, query_block, 0).astype(jnp.float32).reshape(query_block, KVH, group_size, HD)
        key_window = lax.dynamic_slice_in_dim(ext_keys, first_row, window, 0).astype(jnp.float32).reshape(window, KVH, HD)
        value_window = lax.dynamic_slice_in_dim(ext_values, first_row, window, 0).astype(jnp.float32).reshape(window, KVH, HD)
        query_doc = lax.dynamic_slice_in_dim(doc_ids, first_row + rim_rows, query_block, 0)
        key_doc = lax.dynamic_slice_in_dim(doc_ids, first_row, window, 0)
        query_pos = first_row + rim_rows + jnp.arange(query_block, dtype=jnp.int32)
        key_pos = first_row + jnp.arange(window, dtype=jnp.int32)
        allowed = (query_doc[:, None] == key_doc[None, :]) & (key_pos[None, :] <= query_pos[:, None])
        scores = jnp.einsum("qcgd,kcd->cgqk", query_part, key_window) * score_scale
        scores = jnp.where(allowed[None, None], scores, -jnp.inf)
        row_max = jnp.max(scores, axis=-1, keepdims=True)
        raised = jnp.exp(scores - row_max)
        row_sum = jnp.sum(raised, axis=-1)
        probs = lax.optimization_barrier(raised.astype(jnp.bfloat16)).astype(jnp.float32)
        mixed = jnp.einsum("cgqk,kcd->qcgd", probs, value_window)
        mixed = mixed / jnp.transpose(row_sum, (2, 0, 1))[..., None]
        return mixed.astype(jnp.bfloat16).reshape(query_block, QH * HD)

    blocks = lax.map(one_block, jnp.arange(token_count // query_block, dtype=jnp.int32))
    attended = blocks.reshape(token_count, QH * HD)
    feature_width = QH * HD // N_HEADS
    mixed = jnp.zeros((token_count, D_MODEL), jnp.float32)
    for head_group in range(N_HEADS):
        partial_value = jnp.dot(attended[:, head_group * feature_width:(head_group + 1) * feature_width], out_weight[head_group * feature_width:(head_group + 1) * feature_width], preferred_element_type=jnp.float32)
        mixed = mixed + lax.optimization_barrier(partial_value.astype(jnp.bfloat16)).astype(jnp.float32)
    return mixed.astype(jnp.bfloat16)
```

```python
import functools
import jax
import jax.numpy as jnp
from jax import lax
from jax.experimental import pallas as pl
from jax.experimental.pallas import tpu as pltpu
from jax.sharding import PartitionSpec as P

HD = 128
BLOCK = 128
MOSTB = 16
STEP = 4
MASKED = -1e30
EXP2_SCALE = HD ** (-0.5) * 1.4426950408889634


def attend(meta, docs, query, own, other, near, far, out, keys, values, stacked, scores, peak, total):
    tokens = query.shape[0]
    heads = query.shape[1] // HD
    rows = heads * BLOCK
    span = STEP * BLOCK
    shard = meta[0]
    odd = lax.rem(shard, 2)
    blocks = tokens // BLOCK

    def place(index, piece):
        start = pl.multiple_of(index * tokens, BLOCK)
        keys[pl.ds(start, tokens), :] = piece[0]
        values[pl.ds(start, tokens), :HD] = piece[1]

    values[:, HD:] = jnp.ones((values.shape[0], HD), values.dtype)
    place(0, far.at[1])
    place(1, far.at[0])
    place(2, near.at[0])
    place(3, near.at[1])
    place(4 + odd, own)
    place(5 - odd, other)

    def one_block(row, carry):
        place_in = shard * blocks + row
        begin = jnp.int32(0)
        edge = jnp.int32(0)
        for doc in range(docs.shape[0]):
            edge = edge + docs[doc]
            begin = jnp.where(edge <= place_in, edge, begin)
        count = place_in - begin + 1
        steps = lax.div(count + STEP - 1, STEP)
        last = (4 + odd) * blocks + row
        first_row = pl.multiple_of(row * BLOCK, BLOCK)
        for head in range(heads):
            stacked[head * BLOCK : (head + 1) * BLOCK, :] = query[
                pl.ds(first_row, BLOCK), head * HD : (head + 1) * HD
            ]

        def score(step, masked):
            start = pl.multiple_of((last - step * STEP - (STEP - 1)) * BLOCK, BLOCK)
            part = keys[pl.ds(start, span), :]
            column = pl.multiple_of(step * span, span)
            for head in range(heads):
                here = slice(head * BLOCK, (head + 1) * BLOCK)
                got = lax.dot_general(
                    stacked[here, :], part, (((1,), (1,)), ((), ())),
                    preferred_element_type=jnp.float32,
                )
                high = None
                for block in range(STEP):
                    piece = got[:, block * BLOCK : (block + 1) * BLOCK]
                    if masked:
                        back = step * STEP + (STEP - 1 - block)
                        keep = jnp.broadcast_to(back < count, piece.shape)
                        if block == STEP - 1:
                            down = lax.broadcasted_iota(jnp.int32, piece.shape, 0)
                            across = lax.broadcasted_iota(jnp.int32, piece.shape, 1)
                            keep = keep & ((across <= down) | (step > 0))
                        piece = jnp.where(keep, piece, MASKED)
                    scores[here, pl.ds(pl.multiple_of(column + block * BLOCK, BLOCK), BLOCK)] = piece
                    high = piece if high is None else jnp.maximum(high, piece)
                peak[here, :] = jnp.maximum(peak[here, :], high)

        peak[...] = jnp.full(peak.shape, MASKED, jnp.float32)
        score(jnp.int32(0), True)

        def middle(step, carry):
            score(step, False)
            return carry

        lax.fori_loop(1, steps - 1, middle, 0)

        @pl.when(steps > 1)
        def _():
            score(steps - 1, True)

        for head in range(heads):
            here = slice(head * BLOCK, (head + 1) * BLOCK)
            peak[here, :] = jnp.broadcast_to(
                jnp.max(peak[here, :], axis=1, keepdims=True), (BLOCK, BLOCK)
            )
        total[...] = jnp.zeros(total.shape, jnp.float32)

        def weigh(step, carry):
            start = pl.multiple_of((last - step * STEP - (STEP - 1)) * BLOCK, BLOCK)
            part = values[pl.ds(start, span), :]
            column = pl.multiple_of(step * span, span)
            for head in range(heads):
                here = slice(head * BLOCK, (head + 1) * BLOCK)
                top = jnp.concatenate([peak[here, :]] * STEP, axis=1)
                raised = jnp.exp2((scores[here, pl.ds(column, span)] - top) * EXP2_SCALE)
                total[here, :] += jnp.dot(
                    raised.astype(jnp.bfloat16), part, preferred_element_type=jnp.float32
                )
            return carry

        lax.fori_loop(0, steps, weigh, 0)
        for head in range(heads):
            here = slice(head * BLOCK, (head + 1) * BLOCK)
            out[pl.ds(first_row, BLOCK), head * HD : (head + 1) * HD] = (
                total[here, :HD] / total[here, HD:]
            ).astype(out.dtype)
        return carry

    lax.fori_loop(0, blocks, one_block, 0)


def attention(shard, docs, query, own, other, near, far):
    tokens, width = query.shape
    rows = width // HD * BLOCK
    vmem = pl.BlockSpec(memory_space=pltpu.VMEM)
    smem = pl.BlockSpec(memory_space=pltpu.SMEM)
    return pl.pallas_call(
        attend,
        out_shape=jax.ShapeDtypeStruct((tokens, width), jnp.bfloat16),
        in_specs=[smem, smem] + [vmem] * 5,
        out_specs=vmem,
        scratch_shapes=[
            pltpu.VMEM((6 * tokens, HD), jnp.bfloat16),
            pltpu.VMEM((6 * tokens, 2 * HD), jnp.bfloat16),
            pltpu.VMEM((rows, HD), jnp.bfloat16),
            pltpu.VMEM((rows, MOSTB * BLOCK), jnp.float32),
            pltpu.VMEM((rows, BLOCK), jnp.float32),
            pltpu.VMEM((rows, 2 * HD), jnp.float32),
        ],
        name="attend",
    )(shard, docs, query, own, other, near, far)


def project(attended, weight, order):
    tokens, depth = attended.shape
    count = order.shape[0]
    width = weight.shape[1] // 4

    def body(order_ref, left, right, out):
        out[0] = jnp.dot(left[...], right[...], preferred_element_type=jnp.float32).astype(out.dtype)

    return pl.pallas_call(
        body,
        out_shape=jax.ShapeDtypeStruct((count, tokens, width), jnp.bfloat16),
        grid_spec=pltpu.PrefetchScalarGridSpec(
            num_scalar_prefetch=1,
            grid=(count,),
            in_specs=[
                pl.BlockSpec((tokens, depth), lambda i, order: (0, 0)),
                pl.BlockSpec((depth, width), lambda i, order: (0, order[i])),
            ],
            out_specs=pl.BlockSpec((1, tokens, width), lambda i, order: (i, 0, 0)),
        ),
        name="project",
    )(order, attended, weight)


def build(shards, groups):
    def swap_core(block):
        return lax.ppermute(block, "docs", [(i, i ^ 1) for i in range(shards)])

    def exchange(block, first):
        route = []
        for group in range(groups):
            for shard in range(shards):
                flip = 1 if (shard % 2 == 0) == first else 2
                route.append((group * shards + shard, (group ^ flip) * shards + shard))
        return lax.ppermute(block, ("heads", "docs"), route)

    def local(query_rows, key_rows, value_rows, doc_blocks, out_weight):
        shard = lax.axis_index("docs")
        group = lax.axis_index("heads")
        own = jnp.stack([key_rows, value_rows])
        other = swap_core(own)
        pair = jnp.stack([own, other])
        route = []
        for i in range(shards):
            target = i + (4 if i % 2 else 2)
            if target < shards:
                route.append((i, target))
        came = lax.ppermute(pair, "docs", route)
        crossed = swap_core(came)
        odd = shard % 2 == 1
        near = jnp.where(odd, crossed, came)
        far = jnp.where(odd, came, crossed)
        attended = attention(
            jnp.reshape(shard, (1,)).astype(jnp.int32), doc_blocks, query_rows, own, other, near, far
        )
        weight = lax.all_gather(out_weight, "docs", axis=1, tiled=True)
        first = jnp.where(odd, 2, 1)
        second = 3 - first
        send = project(attended, weight, jnp.stack([group ^ first, group ^ 3]).astype(jnp.int32))
        arrived = exchange(send, True)
        keep = project(attended, weight, jnp.stack([group, group ^ second]).astype(jnp.int32))
        f32 = jnp.float32
        onward = (keep[1].astype(f32) + arrived[1].astype(f32)).astype(jnp.bfloat16)
        final = exchange(onward, False)
        return (keep[0].astype(f32) + arrived[0].astype(f32) + final.astype(f32)).astype(jnp.bfloat16)

    return local


def solution(mesh):
    placed = (P("docs", "heads"), P("docs", "heads"), P("docs", "heads"), P(), P("heads", "docs"))
    local = build(mesh.shape["docs"], mesh.shape["heads"])
    return jax.shard_map(
        local, mesh=mesh, in_specs=placed, out_specs=P("docs", "heads"), check_vma=False
    )
```

```python
import functools
import jax
import jax.numpy as jnp
from jax import lax
from jax.experimental import pallas as pl
from jax.experimental.pallas import tpu as pltpu
from jax.sharding import PartitionSpec as P

HD = 128
BLOCK = 128
MOSTB = 16
STEP = 4
MASKED = -1e30
EXP2_SCALE = HD ** (-0.5) * 1.4426950408889634
VMEM = pl.BlockSpec(memory_space=pltpu.VMEM)
SMEM = pl.BlockSpec(memory_space=pltpu.SMEM)
ANY = pl.BlockSpec(memory_space=pl.ANY)


def gather_rows(own, other, near, near_other, far, far_other, keys, values):
    tokens = own.shape[1]
    odd = lax.rem(lax.axis_index("docs"), 2)

    def place(index, piece):
        start = pl.multiple_of(index * tokens, BLOCK)
        keys[pl.ds(start, tokens), :] = piece[0]
        values[pl.ds(start, tokens), :HD] = piece[1]

    values[:, HD:] = jnp.ones((values.shape[0], HD), values.dtype)
    place(0 + odd, far)
    place(1 - odd, far_other)
    place(2 + odd, near)
    place(3 - odd, near_other)
    place(4 + odd, own)
    place(5 - odd, other)


def prepare(pieces):
    rows = len(pieces) * pieces[0].shape[1]
    return pl.pallas_call(
        gather_rows,
        out_shape=(
            jax.ShapeDtypeStruct((rows, HD), jnp.bfloat16),
            jax.ShapeDtypeStruct((rows, 2 * HD), jnp.bfloat16),
        ),
        in_specs=[VMEM] * len(pieces),
        out_specs=(VMEM, VMEM),
        compiler_params=pltpu.CompilerParams(vmem_limit_bytes=12 << 20),
        name="prepare",
    )(*pieces)


def attend(docs, query, keys, values, out, stacked, scores, peak, total, *, first, blocks):
    heads = query.shape[1] // HD
    span = STEP * BLOCK
    shard = lax.axis_index("docs")
    local_blocks = keys.shape[0] // 6 // BLOCK
    odd = lax.rem(shard, 2)

    def one_block(row):
        place_in = shard * local_blocks + first + row
        begin = jnp.int32(0)
        edge = jnp.int32(0)
        for doc in range(docs.shape[0]):
            edge = edge + docs[doc]
            begin = jnp.where(edge <= place_in, edge, begin)
        count = place_in - begin + 1
        steps = lax.div(count + STEP - 1, STEP)
        last = (4 + odd) * local_blocks + first + row
        here_row = pl.multiple_of(row * BLOCK, BLOCK)
        for head in range(heads):
            stacked[head * BLOCK : (head + 1) * BLOCK, :] = query[
                pl.ds(here_row, BLOCK), head * HD : (head + 1) * HD
            ]

        def score(step, masked):
            start = pl.multiple_of((last - step * STEP - (STEP - 1)) * BLOCK, BLOCK)
            part = keys[pl.ds(start, span), :]
            column = pl.multiple_of(step * span, span)
            for head in range(heads):
                here = slice(head * BLOCK, (head + 1) * BLOCK)
                got = lax.dot_general(
                    stacked[here, :], part, (((1,), (1,)), ((), ())),
                    preferred_element_type=jnp.float32,
                )
                high = None
                for block in range(STEP):
                    piece = got[:, block * BLOCK : (block + 1) * BLOCK]
                    if masked:
                        back = step * STEP + (STEP - 1 - block)
                        keep = jnp.broadcast_to(back < count, piece.shape)
                        if block == STEP - 1:
                            down = lax.broadcasted_iota(jnp.int32, piece.shape, 0)
                            across = lax.broadcasted_iota(jnp.int32, piece.shape, 1)
                            keep = keep & ((across <= down) | (step > 0))
                        piece = jnp.where(keep, piece, MASKED)
                    scores[here, pl.ds(pl.multiple_of(column + block * BLOCK, BLOCK), BLOCK)] = piece
                    high = piece if high is None else jnp.maximum(high, piece)
                peak[here, :] = jnp.maximum(peak[here, :], high)

        peak[...] = jnp.full(peak.shape, MASKED, jnp.float32)
        score(jnp.int32(0), True)

        def middle(step, carry):
            score(step, False)
            return carry

        lax.fori_loop(1, steps - 1, middle, 0)

        @pl.when(steps > 1)
        def _():
            score(steps - 1, True)

        for head in range(heads):
            here = slice(head * BLOCK, (head + 1) * BLOCK)
            peak[here, :] = jnp.broadcast_to(
                jnp.max(peak[here, :], axis=1, keepdims=True), (BLOCK, BLOCK)
            )
        total[...] = jnp.zeros(total.shape, jnp.float32)

        def weigh(step, carry):
            start = pl.multiple_of((last - step * STEP - (STEP - 1)) * BLOCK, BLOCK)
            part = values[pl.ds(start, span), :]
            column = pl.multiple_of(step * span, span)
            for head in range(heads):
                here = slice(head * BLOCK, (head + 1) * BLOCK)
                top = jnp.concatenate([peak[here, :]] * STEP, axis=1)
                raised = jnp.exp2((scores[here, pl.ds(column, span)] - top) * EXP2_SCALE)
                total[here, :] += jnp.dot(
                    raised.astype(jnp.bfloat16), part, preferred_element_type=jnp.float32
                )
            return carry

        lax.fori_loop(0, steps, weigh, 0)
        for head in range(heads):
            here = slice(head * BLOCK, (head + 1) * BLOCK)
            out[pl.ds(here_row, BLOCK), head * HD : (head + 1) * HD] = (
                total[here, :HD] / total[here, HD:]
            ).astype(out.dtype)

    for row in range(blocks):
        one_block(row)


def attention(docs, query, keys, values, part, blocks):
    width = query.shape[1]
    rows = width // HD * BLOCK
    return pl.pallas_call(
        functools.partial(attend, first=part * blocks, blocks=blocks),
        out_shape=jax.ShapeDtypeStruct((blocks * BLOCK, width), jnp.bfloat16),
        grid=(1,),
        in_specs=[SMEM, pl.BlockSpec((blocks * BLOCK, width), lambda i: (part, 0)), VMEM, VMEM],
        out_specs=VMEM,
        scratch_shapes=[
            pltpu.VMEM((rows, HD), jnp.bfloat16),
            pltpu.VMEM((rows, MOSTB * BLOCK), jnp.float32),
            pltpu.VMEM((rows, BLOCK), jnp.float32),
            pltpu.VMEM((rows, 2 * HD), jnp.float32),
        ],
        compiler_params=pltpu.CompilerParams(vmem_limit_bytes=24 << 20),
        name="attend",
    )(docs, query, keys, values)


def project(parts, pieces, half):
    part_tokens, depth = parts[0].shape
    tokens = part_tokens * len(parts)
    width = pieces[0].shape[1]
    slots = 4

    def body(*refs):
        lefts, refs = refs[: len(parts)], refs[len(parts) :]
        sources = refs[: len(pieces)]
        outs = refs[len(pieces) : len(pieces) + 2]
        rights, sems = refs[len(pieces) + 2 :]
        shard = lax.axis_index("docs")
        group = lax.axis_index("heads")
        odd = lax.rem(shard, 2)
        plane = lax.div(shard, 2)
        early = jnp.where(odd == 1, 2, 1)
        late = 3 - early
        targets = [group ^ early, group ^ 3, group, group ^ late]
        for slot, target in enumerate(targets):
            distance = jnp.abs(plane - target)
            below = jnp.where(target < plane, 1, 0)
            away = 2 * distance + (below ^ odd)
            index = jnp.where(distance == 0, odd ^ half, away)
            for j, source in enumerate(sources):
                @pl.when(index == j)
                def _(source=source, slot=slot):
                    pltpu.make_async_copy(source, rights.at[slot], sems.at[slot]).start()
        for slot in range(slots):
            pltpu.make_async_copy(sources[0], rights.at[slot], sems.at[slot]).wait()
            for part, left in enumerate(lefts):
                outs[slot // 2][slot % 2, part * part_tokens : (part + 1) * part_tokens, :] = jnp.dot(
                    left[...], rights[slot], preferred_element_type=jnp.float32
                ).astype(jnp.bfloat16)

    shape = jax.ShapeDtypeStruct((2, tokens, width), jnp.bfloat16)
    return pl.pallas_call(
        body,
        out_shape=(shape, shape),
        in_specs=[VMEM] * len(parts) + [ANY] * len(pieces),
        out_specs=(VMEM, VMEM),
        scratch_shapes=[pltpu.VMEM((slots, depth, width), jnp.bfloat16), pltpu.SemaphoreType.DMA((slots,))],
        compiler_params=pltpu.CompilerParams(vmem_limit_bytes=16 << 20),
        name="project",
    )(*parts, *pieces)


def build(shards, groups):
    def send(block, route, axis="docs"):
        return lax.ppermute(block, axis, route)

    swap = [(i, i ^ 1) for i in range(shards)]
    up = [(i, i + 2) for i in range(shards - 2)]
    cross = []
    for i in range(0, shards - 2, 2):
        cross += [(i, i + 3), (i + 3, i)]

    def exchange(block, early):
        route = []
        for group in range(groups):
            for shard in range(shards):
                flip = 1 if (shard % 2 == 0) == early else 2
                route.append((group * shards + shard, (group ^ flip) * shards + shard))
        return send(block, route, ("heads", "docs"))

    def local(query_rows, key_rows, value_rows, doc_blocks, out_weight):
        return inside(query_rows, key_rows, value_rows, doc_blocks, out_weight)

    def inside(query_rows, key_rows, value_rows, doc_blocks, out_weight):
        f32 = jnp.float32
        own = jnp.stack([key_rows, value_rows])
        other = send(own, swap)
        near = send(own, up)
        near_other = send(near, swap)
        far = send(near, up)
        far_other = send(far, swap)
        keys, values = prepare((own, other, near, near_other, far, far_other))
        blocks = own.shape[1] // BLOCK // PARTS
        attended = []
        for part in range(PARTS):
            attended.append(attention(doc_blocks, query_rows, keys, values, part, blocks))

        if shards != 2 * groups:
            weight = lax.all_gather(out_weight, "docs", axis=1, tiled=True)
            partial = jnp.dot(jnp.concatenate(attended), weight, preferred_element_type=f32)
            return lax.psum_scatter(
                partial.astype(jnp.bfloat16), "heads", scatter_dimension=1, tiled=True
            )

        weight_other = send(out_weight, swap)
        pieces = []
        for last in (out_weight, weight_other):
            found = [out_weight, weight_other]
            for _ in range(1, shards // 2):
                got = send(last, cross)
                last = send(got, swap)
                found += [got, last]
            pieces.append(found)
        results = []
        for half in range(2):
            outward, keep = project(attended, pieces[half], half)
            arrived = exchange(outward, True)
            onward = (keep[1].astype(f32) + arrived[1].astype(f32)).astype(jnp.bfloat16)
            final = exchange(onward, False)
            results.append((keep[0].astype(f32) + arrived[0].astype(f32) + final.astype(f32)).astype(jnp.bfloat16))
        ahead = lax.axis_index("heads") > lax.axis_index("docs") // 2
        return jnp.concatenate(
            [jnp.where(ahead, results[1], results[0]), jnp.where(ahead, results[0], results[1])], axis=1
        )

    return local


PARTS = 4


def solution(mesh):
    placed = (P("docs", "heads"), P("docs", "heads"), P("docs", "heads"), P(), P("heads", "docs"))
    shards, groups = mesh.shape["docs"], mesh.shape["heads"]
    return jax.shard_map(
        build(shards, groups), mesh=mesh, in_specs=placed, out_specs=P("docs", "heads"), check_vma=False
    )
```

```python
import functools
import jax
import jax.numpy as jnp
from jax import lax
from jax.experimental import pallas as pl
from jax.experimental.pallas import tpu as pltpu
from jax.sharding import PartitionSpec as P

HD = 128
BLOCK = 128
MOSTB = 16
STEP = 4
TOGETHER = 4
MASKED = -1e30
EXP2_SCALE = HD ** (-0.5) * 1.4426950408889634
VMEM = pl.BlockSpec(memory_space=pltpu.VMEM)
SMEM = pl.BlockSpec(memory_space=pltpu.SMEM)
ANY = pl.BlockSpec(memory_space=pl.ANY)


def gather_rows(own, other, near, near_other, far, far_other, keys, values):
    tokens = own.shape[1]
    odd = lax.rem(lax.axis_index("docs"), 2)

    def place(index, piece):
        start = pl.multiple_of(index * tokens, BLOCK)
        keys[pl.ds(start, tokens), :] = piece[0]
        values[pl.ds(start, tokens), :HD] = piece[1]

    values[:, HD:] = jnp.ones((values.shape[0], HD), values.dtype)
    place(0 + odd, far)
    place(1 - odd, far_other)
    place(2 + odd, near)
    place(3 - odd, near_other)
    place(4 + odd, own)
    place(5 - odd, other)


def prepare(pieces):
    rows = len(pieces) * pieces[0].shape[1]
    return pl.pallas_call(
        gather_rows,
        out_shape=(
            jax.ShapeDtypeStruct((rows, HD), jnp.bfloat16),
            jax.ShapeDtypeStruct((rows, 2 * HD), jnp.bfloat16),
        ),
        in_specs=[VMEM] * len(pieces),
        out_specs=(VMEM, VMEM),
        compiler_params=pltpu.CompilerParams(vmem_limit_bytes=12 << 20),
        name="prepare",
    )(*pieces)


def attend(docs, query, keys, values, *refs, first, heads_together):
    out, scores = refs[-2:]
    heads = query.shape[1] // HD
    rows = heads_together * BLOCK
    shard = lax.axis_index("docs")
    local_blocks = keys.shape[0] // 6 // BLOCK
    place_in = shard * local_blocks + first
    begin = jnp.int32(0)
    edge = jnp.int32(0)
    for doc in range(docs.shape[0]):
        edge = edge + docs[doc]
        begin = jnp.where(edge <= place_in, edge, begin)
    count = place_in - begin + 1
    last = (4 + lax.rem(shard, 2)) * local_blocks + first
    start = pl.multiple_of((last - (MOSTB - 1)) * BLOCK, BLOCK)
    span = STEP * BLOCK
    bias = [jnp.where(MOSTB - 1 - block < count, 0.0, MASKED) for block in range(MOSTB)]
    down = lax.broadcasted_iota(jnp.int32, (rows, BLOCK), 0) % BLOCK
    across = lax.broadcasted_iota(jnp.int32, (rows, BLOCK), 1)
    causal = across <= down

    def score(team):
        slot = team % 2
        left = jnp.concatenate(
            [query[:, h * HD : (h + 1) * HD] for h in range(team * heads_together, (team + 1) * heads_together)]
        )
        high = None
        for chunk in range(MOSTB // STEP):
            got = lax.dot_general(
                left, keys[pl.ds(start + chunk * span, span), :], (((1,), (1,)), ((), ())),
                preferred_element_type=jnp.float32,
            )
            for block in range(STEP):
                number = chunk * STEP + block
                piece = got[:, block * BLOCK : (block + 1) * BLOCK]
                if number == MOSTB - 1:
                    piece = jnp.where(causal, piece, MASKED)
                else:
                    piece = piece + bias[number]
                scores[slot, :, number * BLOCK : (number + 1) * BLOCK] = piece
                high = piece if high is None else jnp.maximum(high, piece)
        return jnp.max(high, axis=1, keepdims=True)

    def weigh(team, top):
        slot = team % 2
        top = jnp.broadcast_to(top, (rows, BLOCK))
        total = None
        for chunk in range(MOSTB // STEP):
            here = slice(chunk * span, (chunk + 1) * span)
            raised = jnp.exp2((scores[slot, :, here] - jnp.concatenate([top] * STEP, axis=1)) * EXP2_SCALE)
            part = jnp.dot(
                raised.astype(jnp.bfloat16), values[pl.ds(start + chunk * span, span), :],
                preferred_element_type=jnp.float32,
            )
            total = part if total is None else total + part
        done = (total[:, :HD] / total[:, HD:]).astype(out.dtype)
        for j in range(heads_together):
            h = team * heads_together + j
            out[:, h * HD : (h + 1) * HD] = done[j * BLOCK : (j + 1) * BLOCK, :]

    teams = heads // heads_together
    top = score(0)
    for team in range(teams):
        following = score(team + 1) if team + 1 < teams else None
        weigh(team, top)
        top = following


def attention(docs, query, keys, values, part, before):
    tokens, width = query.shape
    together = TOGETHER
    return pl.pallas_call(
        functools.partial(attend, first=part, heads_together=together),
        out_shape=jax.ShapeDtypeStruct((tokens, width), jnp.bfloat16),
        grid=(1,),
        in_specs=[SMEM, pl.BlockSpec((BLOCK, width), lambda i: (part, 0)), VMEM, VMEM] + [ANY] * len(before),
        out_specs=pl.BlockSpec((BLOCK, width), lambda i: (part, 0)),
        input_output_aliases={4: 0} if before else {},
        scratch_shapes=[
            pltpu.VMEM((2, together * BLOCK, MOSTB * BLOCK), jnp.float32),
        ],
        compiler_params=pltpu.CompilerParams(vmem_limit_bytes=24 << 20),
        name="attend",
    )(docs, query, keys, values, *before)


def project(attended, pieces, half, first_slot, slots):
    tokens, depth = attended.shape
    width = pieces[0].shape[1]

    def body(left, *refs):
        sources = refs[: len(pieces)]
        out, rights, sems = refs[len(pieces) :]
        shard = lax.axis_index("docs")
        group = lax.axis_index("heads")
        odd = lax.rem(shard, 2)
        plane = lax.div(shard, 2)
        early = jnp.where(odd == 1, 2, 1)
        late = 3 - early
        targets = [group ^ early, group ^ 3, group, group ^ late]
        for slot, target in enumerate(targets[first_slot : first_slot + slots]):
            distance = jnp.abs(plane - target)
            below = jnp.where(target < plane, 1, 0)
            away = 2 * distance + (below ^ odd)
            index = jnp.where(distance == 0, odd ^ half, away)
            for j, source in enumerate(sources):
                @pl.when(index == j)
                def _(source=source, slot=slot):
                    pltpu.make_async_copy(source, rights.at[slot], sems.at[slot]).start()
        for slot in range(slots):
            pltpu.make_async_copy(sources[0], rights.at[slot], sems.at[slot]).wait()
            out[slot] = jnp.dot(
                left[...], rights[slot], preferred_element_type=jnp.float32
            ).astype(jnp.bfloat16)

    shape = jax.ShapeDtypeStruct((slots, tokens, width), jnp.bfloat16)
    return pl.pallas_call(
        body,
        out_shape=shape,
        in_specs=[VMEM] + [ANY] * len(pieces),
        out_specs=VMEM,
        scratch_shapes=[pltpu.VMEM((slots, depth, width), jnp.bfloat16), pltpu.SemaphoreType.DMA((slots,))],
        compiler_params=pltpu.CompilerParams(vmem_limit_bytes=16 << 20),
        name="project",
    )(attended, *pieces)


def build(shards, groups):
    def send(block, route, axis="docs"):
        return lax.ppermute(block, axis, route)

    planes = shards // 2
    swap = [(i, i ^ 1) for i in range(shards)]

    def up(step):
        return [(i, i + 2) for i in range(2 * (step - 1), shards - 2)]

    def cross(step):
        route = []
        for p in range(planes - 1):
            if p >= step - 1:
                route.append((2 * p + (step > 1), 2 * p + 3))
            if p + 1 <= planes - step:
                route.append((2 * p + 2 + (step == 1), 2 * p))
        return route

    def exchange(block, early):
        route = []
        for group in range(groups):
            for shard in range(shards):
                flip = 1 if (shard % 2 == 0) == early else 2
                route.append((group * shards + shard, (group ^ flip) * shards + shard))
        return send(block, route, ("heads", "docs"))

    def local(query_rows, key_rows, value_rows, doc_blocks, out_weight):
        return inside(query_rows, key_rows, value_rows, doc_blocks, out_weight)

    def inside(query_rows, key_rows, value_rows, doc_blocks, out_weight):
        f32 = jnp.float32
        own = jnp.stack([key_rows, value_rows])
        other = send(own, swap)
        near = send(own, up(1))
        near_other = send(near, swap)
        far = send(near, up(2))
        far_other = send(far, swap)
        keys, values = prepare((own, other, near, near_other, far, far_other))
        before = ()
        for part in range(own.shape[1] // BLOCK):
            attended = attention(doc_blocks, query_rows, keys, values, part, before)
            before = (attended,)

        if shards != 2 * groups:
            weight = lax.all_gather(out_weight, "docs", axis=1, tiled=True)
            partial = jnp.dot(attended, weight, preferred_element_type=f32)
            return lax.psum_scatter(
                partial.astype(jnp.bfloat16), "heads", scatter_dimension=1, tiled=True
            )

        weight_other = send(out_weight, swap)
        pieces = []
        for last in (out_weight, weight_other):
            found = [out_weight, weight_other]
            for step in range(1, shards // 2):
                last = send(last, cross(step))
                found += [last, send(last, swap)]
            pieces.append(found)
        results = []
        for half in range(2):
            outward = project(attended, pieces[half], half, 0, 2)
            arrived = exchange(outward, True)
            keep = project(attended, pieces[half], half, 2, 2)
            onward = (keep[1].astype(f32) + arrived[1].astype(f32)).astype(jnp.bfloat16)
            final = exchange(onward, False)
            results.append((keep[0].astype(f32) + arrived[0].astype(f32) + final.astype(f32)).astype(jnp.bfloat16))
        ahead = lax.axis_index("heads") > lax.axis_index("docs") // 2
        return jnp.concatenate(
            [jnp.where(ahead, results[1], results[0]), jnp.where(ahead, results[0], results[1])], axis=1
        )

    return local


def solution(mesh):
    placed = (P("docs", "heads"), P("docs", "heads"), P("docs", "heads"), P(), P("heads", "docs"))
    shards, groups = mesh.shape["docs"], mesh.shape["heads"]
    return jax.shard_map(
        build(shards, groups), mesh=mesh, in_specs=placed, out_specs=P("docs", "heads"), check_vma=False
    )
```

```python
import functools
import jax
import jax.numpy as jnp
from jax import lax
from jax.experimental import pallas as pl
from jax.experimental.pallas import tpu as pltpu
from jax.sharding import PartitionSpec as P

HD = 128
BLOCK = 128
MOSTB = 16
STEP = 4
TOGETHER = 4
MASKED = -1e30
EXP2_SCALE = HD ** (-0.5) * 1.4426950408889634
VMEM = pl.BlockSpec(memory_space=pltpu.VMEM)
SMEM = pl.BlockSpec(memory_space=pltpu.SMEM)
ANY = pl.BlockSpec(memory_space=pl.ANY)


def gather_rows(own, other, near, near_other, far, far_other, keys, values):
    tokens = own.shape[1]
    odd = lax.rem(lax.axis_index("docs"), 2)

    def place(index, piece):
        start = pl.multiple_of(index * tokens, BLOCK)
        keys[pl.ds(start, tokens), :] = piece[0]
        values[pl.ds(start, tokens), :HD] = piece[1]

    values[:, HD:] = jnp.ones((values.shape[0], HD), values.dtype)
    place(0 + odd, far)
    place(1 - odd, far_other)
    place(2 + odd, near)
    place(3 - odd, near_other)
    place(4 + odd, own)
    place(5 - odd, other)


def prepare(pieces):
    rows = len(pieces) * pieces[0].shape[1]
    return pl.pallas_call(
        gather_rows,
        out_shape=(
            jax.ShapeDtypeStruct((rows, HD), jnp.bfloat16),
            jax.ShapeDtypeStruct((rows, 2 * HD), jnp.bfloat16),
        ),
        in_specs=[VMEM] * len(pieces),
        out_specs=(VMEM, VMEM),
        compiler_params=pltpu.CompilerParams(vmem_limit_bytes=12 << 20),
        name="prepare",
    )(*pieces)


def attend(docs, query, keys, values, *refs, first, heads_together):
    out, scores = refs[-2:]
    heads = query.shape[1] // HD
    rows = heads_together * BLOCK
    shard = lax.axis_index("docs")
    local_blocks = keys.shape[0] // 6 // BLOCK
    place_in = shard * local_blocks + first
    begin = jnp.int32(0)
    edge = jnp.int32(0)
    for doc in range(docs.shape[0]):
        edge = edge + docs[doc]
        begin = jnp.where(edge <= place_in, edge, begin)
    count = place_in - begin + 1
    last = (4 + lax.rem(shard, 2)) * local_blocks + first
    start = pl.multiple_of((last - (MOSTB - 1)) * BLOCK, BLOCK)
    span = STEP * BLOCK
    bias = [jnp.where(MOSTB - 1 - block < count, 0.0, MASKED) for block in range(MOSTB)]
    down = lax.broadcasted_iota(jnp.int32, (rows, BLOCK), 0) % BLOCK
    across = lax.broadcasted_iota(jnp.int32, (rows, BLOCK), 1)
    causal = across <= down

    def score(team):
        slot = team % 2
        left = jnp.concatenate(
            [query[:, h * HD : (h + 1) * HD] for h in range(team * heads_together, (team + 1) * heads_together)]
        )
        high = None
        for chunk in range(MOSTB // STEP):
            got = lax.dot_general(
                left, keys[pl.ds(start + chunk * span, span), :], (((1,), (1,)), ((), ())),
                preferred_element_type=jnp.float32,
            )
            for block in range(STEP):
                number = chunk * STEP + block
                piece = got[:, block * BLOCK : (block + 1) * BLOCK]
                if number == MOSTB - 1:
                    piece = jnp.where(causal, piece, MASKED)
                else:
                    piece = piece + bias[number]
                scores[slot, :, number * BLOCK : (number + 1) * BLOCK] = piece
                high = piece if high is None else jnp.maximum(high, piece)
        return jnp.max(high, axis=1, keepdims=True)

    def weigh(team, top):
        slot = team % 2
        top = jnp.broadcast_to(top, (rows, BLOCK))
        total = None
        for chunk in range(MOSTB // STEP):
            here = slice(chunk * span, (chunk + 1) * span)
            raised = jnp.exp2((scores[slot, :, here] - jnp.concatenate([top] * STEP, axis=1)) * EXP2_SCALE)
            part = jnp.dot(
                raised.astype(jnp.bfloat16), values[pl.ds(start + chunk * span, span), :],
                preferred_element_type=jnp.float32,
            )
            total = part if total is None else total + part
        done = (total[:, :HD] / total[:, HD:]).astype(out.dtype)
        for j in range(heads_together):
            h = team * heads_together + j
            out[:, h * HD : (h + 1) * HD] = done[j * BLOCK : (j + 1) * BLOCK, :]

    teams = heads // heads_together
    top = score(0)
    for team in range(teams):
        following = score(team + 1) if team + 1 < teams else None
        weigh(team, top)
        top = following


def attention(docs, query, keys, values, part, before):
    tokens, width = query.shape
    together = TOGETHER
    return pl.pallas_call(
        functools.partial(attend, first=part, heads_together=together),
        out_shape=jax.ShapeDtypeStruct((tokens, width), jnp.bfloat16),
        grid=(1,),
        in_specs=[SMEM, pl.BlockSpec((BLOCK, width), lambda i: (part, 0)), VMEM, VMEM] + [ANY] * len(before),
        out_specs=pl.BlockSpec((BLOCK, width), lambda i: (part, 0)),
        input_output_aliases={4: 0} if before else {},
        scratch_shapes=[
            pltpu.VMEM((2, together * BLOCK, MOSTB * BLOCK), jnp.float32),
        ],
        compiler_params=pltpu.CompilerParams(vmem_limit_bytes=24 << 20),
        name="attend",
    )(docs, query, keys, values, *before)


def project(attended, pieces, half, first_slot, slots):
    tokens, _ = attended.shape
    width = pieces[0].shape[1]

    def body(left, *refs):
        sources, out = refs[:-1], refs[-1]
        shard = lax.axis_index("docs")
        group = lax.axis_index("heads")
        odd = lax.rem(shard, 2)
        plane = lax.div(shard, 2)
        early = jnp.where(odd == half, 2, 1)
        late = 3 - early
        targets = [group ^ early, group ^ 3, group, group ^ late][first_slot : first_slot + slots]

        def one_slot(slot, carry):
            target = jnp.where(slot == 0, targets[0], targets[1])
            distance = jnp.abs(plane - target)
            arrived_on_odd = jnp.where((target < plane) | (distance > 1), 1, 0)
            away = 2 * distance + (arrived_on_odd ^ odd)
            index = jnp.where(distance == 0, odd ^ half, away)
            for j, source in enumerate(sources):
                @pl.when(index == j)
                def _(source=source):
                    out[slot] = jnp.dot(
                        left[...], source[...], preferred_element_type=jnp.float32
                    ).astype(jnp.bfloat16)
            return carry

        lax.fori_loop(0, slots, one_slot, 0)

    return pl.pallas_call(
        body,
        out_shape=jax.ShapeDtypeStruct((slots, tokens, width), jnp.bfloat16),
        in_specs=[VMEM] * (1 + len(pieces)),
        out_specs=VMEM,
        compiler_params=pltpu.CompilerParams(vmem_limit_bytes=16 << 20),
        name="project",
    )(attended, *pieces)


def build(shards, groups):
    def send(block, route, axis="docs"):
        return lax.ppermute(block, axis, route)

    planes = shards // 2
    swap = [(i, i ^ 1) for i in range(shards)]

    def up(step):
        return [(i, i + 2) for i in range(2 * (step - 1), shards - 2)]

    def cross(step):
        route = []
        for p in range(planes - 1):
            if p >= step - 1:
                route.append((2 * p + (step > 1), 2 * p + 3))
            if p + 1 <= planes - step:
                route.append((2 * p + 2 + (step != 2), 2 * p + (step > 1)))
        return route

    def exchange(block, early):
        route = []
        for group in range(groups):
            for shard in range(shards):
                flip = 1 if (shard % 2 == 0) == early else 2
                route.append((group * shards + shard, (group ^ flip) * shards + shard))
        return send(block, route, ("heads", "docs"))

    def local(query_rows, key_rows, value_rows, doc_blocks, out_weight):
        return inside(query_rows, key_rows, value_rows, doc_blocks, out_weight)

    def inside(query_rows, key_rows, value_rows, doc_blocks, out_weight):
        f32 = jnp.float32
        own = jnp.stack([key_rows, value_rows])
        other = send(own, swap)
        near = send(own, up(1))
        near_other = send(near, swap)
        far = send(near, up(2))
        far_other = send(far, swap)
        keys, values = prepare((own, other, near, near_other, far, far_other))
        before = ()
        for part in range(own.shape[1] // BLOCK):
            attended = attention(doc_blocks, query_rows, keys, values, part, before)
            before = (attended,)

        if shards != 2 * groups:
            weight = lax.all_gather(out_weight, "docs", axis=1, tiled=True)
            partial = jnp.dot(attended, weight, preferred_element_type=f32)
            return lax.psum_scatter(
                partial.astype(jnp.bfloat16), "heads", scatter_dimension=1, tiled=True
            )

        weight_other = send(out_weight, swap)
        pieces = []
        for last in (out_weight, weight_other):
            found = [out_weight, weight_other]
            for step in range(1, shards // 2):
                last = send(last, cross(step))
                found += [last, send(last, swap)]
            pieces.append(found)
        results = []
        for half in range(2):
            outward = project(attended, pieces[half], half, 0, 2)
            arrived = exchange(outward, half == 1)
            keep = project(attended, pieces[half], half, 2, 2)
            onward = (keep[1].astype(f32) + arrived[1].astype(f32)).astype(jnp.bfloat16)
            final = exchange(onward, half == 0)
            results.append((keep[0].astype(f32) + arrived[0].astype(f32) + final.astype(f32)).astype(jnp.bfloat16))
        half_width = results[0].shape[1]
        ahead = (lax.axis_index("heads") > lax.axis_index("docs") // 2).astype(jnp.int32)
        mixed = jnp.zeros((results[0].shape[0], 2 * half_width), jnp.bfloat16)
        mixed = lax.dynamic_update_slice(mixed, results[0], (0, ahead * half_width))
        mixed = lax.optimization_barrier(mixed)
        return lax.dynamic_update_slice(mixed, results[1], (0, (1 - ahead) * half_width))

    return local


def solution(mesh):
    placed = (P("docs", "heads"), P("docs", "heads"), P("docs", "heads"), P(), P("heads", "docs"))
    shards, groups = mesh.shape["docs"], mesh.shape["heads"]
    return jax.shard_map(
        build(shards, groups), mesh=mesh, in_specs=placed, out_specs=P("docs", "heads"), check_vma=False
    )
```

```python
import functools
import jax
import jax.numpy as jnp
from jax import lax
from jax.experimental import pallas as pl
from jax.experimental.pallas import tpu as pltpu
from jax.sharding import PartitionSpec as P

HD = 128
BLOCK = 128
MOSTB = 16
STEP = 4
TOGETHER = 4
MASKED = -1e30
EXP2_SCALE = HD ** (-0.5) * 1.4426950408889634
VMEM = pl.BlockSpec(memory_space=pltpu.VMEM)
SMEM = pl.BlockSpec(memory_space=pltpu.SMEM)
ANY = pl.BlockSpec(memory_space=pl.ANY)


def gather_rows(own, other, near, near_other, far, far_other, keys, values):
    tokens = own.shape[1]
    odd = lax.rem(lax.axis_index("docs"), 2)

    def place(index, piece):
        start = pl.multiple_of(index * tokens, BLOCK)
        keys[pl.ds(start, tokens), :] = piece[0]
        values[pl.ds(start, tokens), :HD] = piece[1]

    values[:, HD:] = jnp.ones((values.shape[0], HD), values.dtype)
    place(0 + odd, far)
    place(1 - odd, far_other)
    place(2 + odd, near)
    place(3 - odd, near_other)
    place(4 + odd, own)
    place(5 - odd, other)


def prepare(pieces):
    rows = len(pieces) * pieces[0].shape[1]
    return pl.pallas_call(
        gather_rows,
        out_shape=(
            jax.ShapeDtypeStruct((rows, HD), jnp.bfloat16),
            jax.ShapeDtypeStruct((rows, 2 * HD), jnp.bfloat16),
        ),
        in_specs=[VMEM] * len(pieces),
        out_specs=(VMEM, VMEM),
        compiler_params=pltpu.CompilerParams(vmem_limit_bytes=12 << 20),
        name="prepare",
    )(*pieces)


def attend(docs, query, keys, values, *refs, first, heads_together):
    out, scores = refs[-2:]
    heads = query.shape[1] // HD
    rows = heads_together * BLOCK
    shard = lax.axis_index("docs")
    local_blocks = keys.shape[0] // 6 // BLOCK
    place_in = shard * local_blocks + first
    begin = jnp.int32(0)
    edge = jnp.int32(0)
    for doc in range(docs.shape[0]):
        edge = edge + docs[doc]
        begin = jnp.where(edge <= place_in, edge, begin)
    count = place_in - begin + 1
    last = (4 + lax.rem(shard, 2)) * local_blocks + first

    def run(window):
        start = pl.multiple_of((last - (window - 1)) * BLOCK, BLOCK)
        span = STEP * BLOCK
        bias = [jnp.where(window - 1 - block < count, 0.0, MASKED) for block in range(window)]
        down = lax.broadcasted_iota(jnp.int32, (rows, BLOCK), 0) % BLOCK
        across = lax.broadcasted_iota(jnp.int32, (rows, BLOCK), 1)
        causal = across <= down

        def score(team):
            slot = team % 2
            left = jnp.concatenate(
                [query[:, h * HD : (h + 1) * HD] for h in range(team * heads_together, (team + 1) * heads_together)]
            )
            high = None
            for chunk in range(window // STEP):
                got = lax.dot_general(
                    left, keys[pl.ds(start + chunk * span, span), :], (((1,), (1,)), ((), ())),
                    preferred_element_type=jnp.float32,
                )
                for block in range(STEP):
                    number = chunk * STEP + block
                    piece = got[:, block * BLOCK : (block + 1) * BLOCK]
                    if number == window - 1:
                        piece = jnp.where(causal, piece, MASKED)
                    else:
                        piece = piece + bias[number]
                    scores[slot, :, number * BLOCK : (number + 1) * BLOCK] = piece
                    high = piece if high is None else jnp.maximum(high, piece)
            return jnp.max(high, axis=1, keepdims=True)

        def weigh(team, top):
            slot = team % 2
            top = jnp.broadcast_to(top, (rows, BLOCK))
            total = None
            for chunk in range(window // STEP):
                here = slice(chunk * span, (chunk + 1) * span)
                raised = jnp.exp2((scores[slot, :, here] - jnp.concatenate([top] * STEP, axis=1)) * EXP2_SCALE)
                part = jnp.dot(
                    raised.astype(jnp.bfloat16), values[pl.ds(start + chunk * span, span), :],
                    preferred_element_type=jnp.float32,
                )
                total = part if total is None else total + part
            done = (total[:, :HD] / total[:, HD:]).astype(out.dtype)
            for j in range(heads_together):
                h = team * heads_together + j
                out[:, h * HD : (h + 1) * HD] = done[j * BLOCK : (j + 1) * BLOCK, :]

        teams = heads // heads_together
        top = score(0)
        for team in range(teams):
            following = score(team + 1) if team + 1 < teams else None
            weigh(team, top)
            top = following

    @pl.when(count <= MOSTB // 2)
    def _():
        run(MOSTB // 2)

    @pl.when(count > MOSTB // 2)
    def _():
        run(MOSTB)


def attention(docs, query, keys, values, part, before):
    tokens, width = query.shape
    together = TOGETHER
    return pl.pallas_call(
        functools.partial(attend, first=part, heads_together=together),
        out_shape=jax.ShapeDtypeStruct((tokens, width), jnp.bfloat16),
        grid=(1,),
        in_specs=[SMEM, pl.BlockSpec((BLOCK, width), lambda i: (part, 0)), VMEM, VMEM] + [ANY] * len(before),
        out_specs=pl.BlockSpec((BLOCK, width), lambda i: (part, 0)),
        input_output_aliases={4: 0} if before else {},
        scratch_shapes=[
            pltpu.VMEM((2, together * BLOCK, MOSTB * BLOCK), jnp.float32),
        ],
        compiler_params=pltpu.CompilerParams(vmem_limit_bytes=24 << 20),
        name="attend",
    )(docs, query, keys, values, *before)


def project(attended, pieces, half, first_slot, slots):
    tokens, _ = attended.shape
    width = pieces[0].shape[1]

    def body(left, *refs):
        sources, out = refs[:-1], refs[-1]
        shard = lax.axis_index("docs")
        group = lax.axis_index("heads")
        odd = lax.rem(shard, 2)
        plane = lax.div(shard, 2)
        early = jnp.where(odd == half, 2, 1)
        late = 3 - early
        targets = [group ^ early, group ^ 3, group, group ^ late][first_slot : first_slot + slots]

        def one_slot(slot, carry):
            target = jnp.where(slot == 0, targets[0], targets[1])
            distance = jnp.abs(plane - target)
            arrived_on_odd = jnp.where((target < plane) | (distance > 1), 1, 0)
            away = 2 * distance + (arrived_on_odd ^ odd)
            index = jnp.where(distance == 0, odd ^ half, away)
            for j, source in enumerate(sources):
                @pl.when(index == j)
                def _(source=source):
                    out[slot] = jnp.dot(
                        left[...], source[...], preferred_element_type=jnp.float32
                    ).astype(jnp.bfloat16)
            return carry

        lax.fori_loop(0, slots, one_slot, 0)

    return pl.pallas_call(
        body,
        out_shape=jax.ShapeDtypeStruct((slots, tokens, width), jnp.bfloat16),
        in_specs=[VMEM] * (1 + len(pieces)),
        out_specs=VMEM,
        compiler_params=pltpu.CompilerParams(vmem_limit_bytes=16 << 20),
        name="project",
    )(attended, *pieces)


def build(shards, groups):
    def send(block, route, axis="docs"):
        return lax.ppermute(block, axis, route)

    planes = shards // 2
    swap = [(i, i ^ 1) for i in range(shards)]

    def up(step):
        return [(i, i + 2) for i in range(2 * (step - 1), shards - 2)]

    def cross(step):
        route = []
        for p in range(planes - 1):
            if p >= step - 1:
                route.append((2 * p + (step > 1), 2 * p + 3))
            if p + 1 <= planes - step:
                route.append((2 * p + 2 + (step != 2), 2 * p + (step > 1)))
        return route

    def exchange(block, early):
        route = []
        for group in range(groups):
            for shard in range(shards):
                flip = 1 if (shard % 2 == 0) == early else 2
                route.append((group * shards + shard, (group ^ flip) * shards + shard))
        return send(block, route, ("heads", "docs"))

    def local(query_rows, key_rows, value_rows, doc_blocks, out_weight):
        return inside(query_rows, key_rows, value_rows, doc_blocks, out_weight)

    def inside(query_rows, key_rows, value_rows, doc_blocks, out_weight):
        f32 = jnp.float32
        own = jnp.stack([key_rows, value_rows])
        other = send(own, swap)
        near = send(own, up(1))
        near_other = send(near, swap)
        far = send(near, up(2))
        far_other = send(far, swap)
        keys, values = prepare((own, other, near, near_other, far, far_other))
        before = ()
        for part in range(own.shape[1] // BLOCK):
            attended = attention(doc_blocks, query_rows, keys, values, part, before)
            before = (attended,)

        if shards != 2 * groups:
            weight = lax.all_gather(out_weight, "docs", axis=1, tiled=True)
            partial = jnp.dot(attended, weight, preferred_element_type=f32)
            return lax.psum_scatter(
                partial.astype(jnp.bfloat16), "heads", scatter_dimension=1, tiled=True
            )

        weight_other = send(out_weight, swap)
        pieces = []
        for last in (out_weight, weight_other):
            found = [out_weight, weight_other]
            for step in range(1, shards // 2):
                last = send(last, cross(step))
                found += [last, send(last, swap)]
            pieces.append(found)
        results = []
        for half in range(2):
            outward = project(attended, pieces[half], half, 0, 2)
            arrived = exchange(outward, half == 1)
            keep = project(attended, pieces[half], half, 2, 2)
            early_sum = lax.optimization_barrier(keep[0].astype(f32) + arrived[0].astype(f32))
            onward = (keep[1].astype(f32) + arrived[1].astype(f32)).astype(jnp.bfloat16)
            final = exchange(onward, half == 0)
            results.append((early_sum + final.astype(f32)).astype(jnp.bfloat16))
        half_width = results[0].shape[1]
        ahead = (lax.axis_index("heads") > lax.axis_index("docs") // 2).astype(jnp.int32)
        mixed = jnp.zeros((results[0].shape[0], 2 * half_width), jnp.bfloat16)
        mixed = lax.dynamic_update_slice(mixed, results[0], (0, ahead * half_width))
        mixed = lax.optimization_barrier(mixed)
        return lax.dynamic_update_slice(mixed, results[1], (0, (1 - ahead) * half_width))

    return local


def solution(mesh):
    placed = (P("docs", "heads"), P("docs", "heads"), P("docs", "heads"), P(), P("heads", "docs"))
    shards, groups = mesh.shape["docs"], mesh.shape["heads"]
    return jax.shard_map(
        build(shards, groups), mesh=mesh, in_specs=placed, out_specs=P("docs", "heads"), check_vma=False
    )
```
